32 devices in a mesh: groups: 2 (over x), pool: 2 (over core), tensor: 8 (over z, y).
Axes of the slice: x: 2, y: 2, z: 4, core: 2. Of those that a mesh axis runs over, the one named last changes fastest.
Arguments:
- hidden: bfloat16 [64, 5120], P(('groups', 'pool', 'tensor')), parts along dimension 0, may hold values from -1.5 to 1.5
- input_gain: float32 [5120], replicated, may hold values from 0.1 to 1.9
- query_weight: bfloat16 [5120, 4096], P(None, ('pool', 'tensor')), may hold values from -0.078125 to 0.078125
- key_weight: bfloat16 [5120, 512], P(None, ('pool', 'tensor')), may hold values from -0.078125 to 0.078125
- value_weight: bfloat16 [5120, 512], P(None, ('pool', 'tensor')), may hold values from -0.078125 to 0.078125
- query_gain: float32 [128], replicated, may hold values from 2 to 6
- key_gain: float32 [128], replicated, may hold values from 1 to 4
- output_weight: bfloat16 [4096, 5120], P(('pool', 'tensor')), may hold values from -0.09375 to 0.09375
- post_gain: float32 [5120], replicated, may hold values from 0.1 to 1.9
- gate_weight: bfloat16 [5120, 12800], P(None, ('pool', 'tensor')), may hold values from -0.078125 to 0.078125
- up_weight: bfloat16 [5120, 12800], P(None, ('pool', 'tensor')), may hold values from -0.078125 to 0.078125
- down_weight: bfloat16 [12800, 5120], P(('pool', 'tensor')), may hold values from -0.0546875 to 0.0546875
- key_cache: bfloat16 [65536, 512], P(('groups', 'pool', 'tensor')), parts along dimension 0, may hold values from -45 to 45
- value_cache: bfloat16 [65536, 512], P(('groups', 'pool', 'tensor')), parts along dimension 0, may hold values from -6 to 6
- lengths: int32 [64], P('groups'), parts along dimension 0, may hold values from 128 to 2048, as said below
- request_slot: int32 [64], P('groups'), parts along dimension 0, may hold values from 0 to 63, as said below
Outputs:
- mixed: bfloat16 [64, 5120], P(('groups', 'pool', 'tensor')), parts along dimension 0
- final: bfloat16 [64, 5120], P(('groups', 'pool', 'tensor')), parts along dimension 0
The draws below stay inside these ranges and needn't reach their ends.
There are 2 independent parts, one for each index of `groups`. The reference program is written for one: setup_inputs(seed, part) draws one part's arguments, and reference() takes and returns one part's arrays. A program takes and returns all parts, laid end to end along the dimension named above; an argument that names none is the same for every part. Nothing has to cross between parts.
Inputs may be any that keep to these rules, and one draw needn't show every extreme that they name: `request_slot`: each owner holds at most 4 requests and some owner holds exactly 4; no two requests share a slot. The lengths of one owner's requests sum to at most 2048; some request has exactly 2048 and some exactly 128.
All inputs are finite; a program needn't handle non-finite values.
Results may differ from the reference program's by a relative error of at most 0.03.
The reference program's roundings to bfloat16 on the way count: a program that leaves them out, or rounds other values in their place, can miss the bound.
Values may be sent and summed in bfloat16 or wider, within the bound.
A program may use at most 64 MiB of HBM per device.

```python
import math
import jax
import jax.numpy as jnp
from jax import lax

D = 5120
HEADS = 32
KV_HEADS = 4
HD = 128
FF = 12800
SLOTS = 4
MAXLEN = 2048
MINLEN = 128
OWNERS = 16
REQ = 32
QD = 4096
KD = 512


def request_layout(key):
    folded = jax.random.fold_in(key, 7)
    key_owner, key_length, key_order = jax.random.split(folded, 3)
    pattern = jnp.tile(jnp.array([4, 1, 2, 1], jnp.int32), OWNERS // 4)
    owner_order = jax.random.permutation(key_owner, OWNERS)
    counts = jnp.zeros((OWNERS,), jnp.int32).at[owner_order].set(pattern)
    slot_ids = jnp.arange(OWNERS * SLOTS, dtype=jnp.int32)
    usable = slot_ids % SLOTS < counts[slot_ids // SLOTS]
    ranked = jnp.sort(jnp.where(usable, slot_ids, slot_ids + OWNERS * SLOTS))[:REQ]
    chosen = ranked[jax.random.permutation(key_order, REQ)]
    holders = counts[chosen // SLOTS]
    ceiling = MAXLEN // holders
    length_draw = jax.random.randint(key_length, (REQ,), MINLEN, ceiling + 1)
    length_draw = jnp.where(chosen == owner_order[1] * SLOTS, MAXLEN, length_draw)
    length_draw = jnp.where(chosen == owner_order[0] * SLOTS, MINLEN, length_draw)
    return (chosen.astype(jnp.int32), length_draw.astype(jnp.int32))


def draw_request_slot(key, part):
    return request_layout(key)[0]


def draw_lengths(key, part):
    return request_layout(key)[1]


def draw_key_cache(key, part):
    row_total = OWNERS * MAXLEN
    drawn = jnp.clip(jax.random.normal(jax.random.fold_in(key, 13), (row_total, KV_HEADS * HD), jnp.float32), -6.0, 6.0)
    return drawn.astype(jnp.bfloat16)


def level_of(key, extent, cuts, least, top_value):
    level, own = 1.0, jax.random.fold_in(key, 6)
    for dim, shards_of in cuts:
        steps = jnp.exp(jax.random.uniform(jax.random.fold_in(own, dim), (shards_of,), jnp.float32, least / len(cuts), top_value / len(cuts)))
        level = level * jnp.repeat(steps, extent[dim] // shards_of).reshape([-1 if axis == dim else 1 for axis in range(len(extent))])
    return level


def scatter_about(key, dims, deviation, limit, pieces=(), kind=jnp.bfloat16):
    result = deviation * jax.random.normal(key, dims, jnp.float32)
    if pieces:
        result = result * level_of(key, dims, pieces, -0.22, 0.18)
    return jnp.clip(result, -limit, limit).astype(kind)


def setup_inputs(seed: int = 0, part: int = 0) -> dict:
    splits = jax.random.split(jax.random.key(seed), 17)
    part_splits = jax.random.split(jax.random.fold_in(splits[16], part), 17)
    return {
        "hidden": scatter_about(part_splits[0], (REQ, D), 0.25, 1.5, ((0, 16),)),
        "input_gain": jnp.clip(1.0 + 0.18 * jax.random.normal(splits[1], (D,), jnp.float32), 0.1, 1.9),
        "query_weight": scatter_about(splits[2], (D, QD), D ** -0.5, 0.078125, ((1, 16),)),
        "key_weight": scatter_about(splits[3], (D, KD), D ** -0.5, 0.078125, ((1, 16),)),
        "value_weight": scatter_about(splits[4], (D, KD), D ** -0.5, 0.078125, ((1, 16),)),
        "query_gain": jnp.clip(jnp.exp(jax.random.uniform(splits[5], (HD,), jnp.float32, math.log(2.0), math.log(6.0))), 2.0, 6.0),
        "key_gain": jnp.clip(jnp.exp(jax.random.uniform(splits[6], (HD,), jnp.float32, math.log(1.0), math.log(4.0))), 1.0, 4.0),
        "output_weight": scatter_about(splits[7], (QD, D), QD ** -0.5, 0.09375, ((0, 16),)),
        "post_gain": jnp.clip(1.0 + 0.18 * jax.random.normal(splits[8], (D,), jnp.float32), 0.1, 1.9),
        "gate_weight": scatter_about(splits[9], (D, FF), D ** -0.5, 0.078125, ((1, 16),)),
        "up_weight": scatter_about(splits[10], (D, FF), D ** -0.5, 0.078125, ((1, 16),)),
        "down_weight": scatter_about(splits[11], (FF, D), FF ** -0.5, 0.0546875, ((0, 16),)),
        "key_cache": draw_key_cache(jax.random.fold_in(jax.random.fold_in(splits[16], part), 71), part),
        "value_cache": scatter_about(part_splits[13], (OWNERS * MAXLEN, KD), 1.0, 6.0, ((0, 16),)),
        "lengths": draw_lengths(jax.random.fold_in(jax.random.fold_in(splits[16], part), 71), part),
        "request_slot": draw_request_slot(jax.random.fold_in(jax.random.fold_in(splits[16], part), 71), part),
    }


eps = 1e-06
theta = 1000000.0

def rms_scale(values, scales):
    values = values.astype(jnp.float32)
    return values * lax.rsqrt(lax.optimization_barrier(jnp.mean(values * values, axis=-1, keepdims=True)) + eps) * scales

def rotate(values, position):
    half_width = values.shape[-1] // 2
    frequency = theta ** (-jnp.arange(half_width, dtype=jnp.float32) * 2.0 / values.shape[-1])
    angles = position * frequency
    cosine = jnp.cos(angles)
    sine_part = jnp.sin(angles)
    front_half = values[..., :half_width]
    back_half = values[..., half_width:]
    return jnp.concatenate([front_half * cosine - back_half * sine_part, back_half * cosine + front_half * sine_part], axis=-1)

def reference(hidden, input_gain, query_weight, key_weight, value_weight, query_gain, key_gain, output_weight, post_gain, gate_weight, up_weight, down_weight, key_cache, value_cache, lengths, request_slot):
    requests = hidden.shape[0]
    group_size = HEADS // KV_HEADS
    normed = rms_scale(hidden, input_gain).astype(jnp.bfloat16)
    query_rows = jnp.dot(normed, query_weight, preferred_element_type=jnp.float32).astype(jnp.bfloat16)
    key_rows = jnp.dot(normed, key_weight, preferred_element_type=jnp.float32).astype(jnp.bfloat16)
    value_rows = jnp.dot(normed, value_weight, preferred_element_type=jnp.float32).astype(jnp.bfloat16)
    position = lengths.astype(jnp.float32)[:, None, None]
    query_heads = rotate(rms_scale(query_rows.reshape(requests, HEADS, HD), query_gain), position).astype(jnp.bfloat16)
    query_heads = query_heads.reshape(requests, KV_HEADS, group_size, HD)
    key_new = rotate(rms_scale(key_rows.reshape(requests, KV_HEADS, HD), key_gain), position).astype(jnp.bfloat16)
    value_new = value_rows.reshape(requests, KV_HEADS, HD)
    owner_of = (request_slot // SLOTS).astype(jnp.int32)
    within = request_slot % SLOTS
    earlier = (owner_of[None, :] == owner_of[:, None]) & (within[None, :] < within[:, None])
    offsets = lax.optimization_barrier(jnp.sum(jnp.where(earlier, lengths[None, :], 0), axis=1)).astype(jnp.int32)
    pooled_keys = key_cache.reshape(OWNERS, MAXLEN, KV_HEADS, HD)
    pooled_values = value_cache.reshape(OWNERS, MAXLEN, KV_HEADS, HD)
    token_pos = jnp.arange(MAXLEN, dtype=jnp.int32)
    scale_factor = 1.0 / math.sqrt(HD)

    def attend(items):
        query_one, key_one, value_one, owner_one, offset_one, length_one = items
        keys_here = lax.dynamic_index_in_dim(pooled_keys, owner_one, 0, keepdims=False).astype(jnp.float32)
        values_here = lax.dynamic_index_in_dim(pooled_values, owner_one, 0, keepdims=False).astype(jnp.float32)
        query_float = query_one.astype(jnp.float32)
        scores = jnp.einsum('kgd,tkd->kgt', query_float, keys_here) * scale_factor
        own_score = jnp.einsum('kgd,kd->kg', query_float, key_one.astype(jnp.float32)) * scale_factor
        inside = ((token_pos >= offset_one) & (token_pos < offset_one + length_one))[None, None, :]
        largest = jnp.maximum(lax.optimization_barrier(jnp.max(jnp.where(inside, scores, -1e+30), axis=2)), own_score)
        weights = jnp.where(inside, jnp.exp(scores - largest[..., None]), 0.0)
        own_weight = jnp.exp(own_score - largest)
        denominator = lax.optimization_barrier(jnp.sum(weights, axis=2)) + own_weight
        weights_low = weights.astype(jnp.bfloat16).astype(jnp.float32)
        own_low = own_weight.astype(jnp.bfloat16).astype(jnp.float32)
        summed = jnp.einsum('kgt,tkd->kgd', weights_low, values_here)
        summed = summed + own_low[..., None] * value_one.astype(jnp.float32)[:, None, :]
        return (summed / denominator[..., None]).astype(jnp.bfloat16).reshape(HEADS * HD)
    head_rows = lax.map(attend, (query_heads, key_new, value_new, owner_of, offsets, lengths.astype(jnp.int32)))
    attended = jnp.dot(head_rows, output_weight, preferred_element_type=jnp.float32)
    mixed = (hidden.astype(jnp.float32) + attended).astype(jnp.bfloat16)
    post_normed = rms_scale(mixed, post_gain).astype(jnp.bfloat16)
    gate_part = jnp.dot(post_normed, gate_weight, preferred_element_type=jnp.float32)
    up_part = jnp.dot(post_normed, up_weight, preferred_element_type=jnp.float32)
    activated = (jax.nn.silu(gate_part) * up_part).astype(jnp.bfloat16)
    lowered = jnp.dot(activated, down_weight, preferred_element_type=jnp.float32)
    final = (mixed.astype(jnp.float32) + lowered).astype(jnp.bfloat16)
    return (mixed, final)
```

```python
import functools
import math

import jax
import jax.numpy as jnp
from jax import lax
from jax.experimental import pallas as pl
from jax.experimental.pallas import tpu as pltpu
from jax.sharding import PartitionSpec as P

SLOTS = 4


eps = 1e-06
theta = 1000000.0


def rms_scale(values, scales):
    values = values.astype(jnp.float32)
    return values * lax.rsqrt(jnp.mean(values * values, axis=-1, keepdims=True) + eps) * scales


def rotate(values, position):
    half_width = values.shape[-1] // 2
    frequency = theta ** (-jnp.arange(half_width, dtype=jnp.float32) * 2.0 / values.shape[-1])
    angles = position * frequency
    cosine = jnp.cos(angles)
    sine_part = jnp.sin(angles)
    front_half = values[..., :half_width]
    back_half = values[..., half_width:]
    return jnp.concatenate(
        [front_half * cosine - back_half * sine_part, back_half * cosine + front_half * sine_part],
        axis=-1,
    )


def on_device(
    hidden,
    input_gain,
    query_weight,
    key_weight,
    value_weight,
    query_gain,
    key_gain,
    output_weight,
    post_gain,
    gate_weight,
    up_weight,
    down_weight,
    key_cache,
    value_cache,
    lengths,
    request_slot,
):
    devices = lax.axis_size(("pool", "tensor"))
    device_index = lax.axis_index(("pool", "tensor"))
    local_rows = hidden.shape[0]
    query_cols = query_weight.shape[1]
    key_cols = key_weight.shape[1]
    width_sent = query_cols + 2 * key_cols
    head_dim = query_gain.shape[0]
    slot_count = SLOTS
    head_count = devices * query_cols // head_dim
    kv_count = devices * key_cols // head_dim
    group_size = head_count // kv_count
    normed = rms_scale(hidden, input_gain).astype(jnp.bfloat16)
    shard_rows = lax.all_gather(normed, ("pool", "tensor"), axis=0, tiled=True)
    query_part = jnp.dot(shard_rows, query_weight, preferred_element_type=jnp.float32)
    key_part = jnp.dot(shard_rows, key_weight, preferred_element_type=jnp.float32)
    value_part = jnp.dot(shard_rows, value_weight, preferred_element_type=jnp.float32)
    projected = jnp.concatenate([query_part, key_part, value_part], axis=1).astype(jnp.bfloat16)
    outgoing = (
        jnp.zeros((devices * slot_count, width_sent), jnp.bfloat16).at[request_slot].set(projected)
    )
    outgoing = outgoing.reshape(devices, slot_count, width_sent)
    arrived = lax.all_to_all(
        outgoing, ("pool", "tensor"), split_axis=0, concat_axis=2, tiled=True
    ).reshape(slot_count, devices, width_sent)
    query_full = arrived[:, :, :query_cols].reshape(slot_count, head_count, head_dim)
    key_full = arrived[:, :, query_cols : query_cols + key_cols].reshape(
        slot_count, kv_count, head_dim
    )
    value_new = arrived[:, :, query_cols + key_cols :].reshape(slot_count, kv_count, head_dim)
    slot_ids = device_index * slot_count + jnp.arange(slot_count, dtype=jnp.int32)
    matches = request_slot[None, :] == slot_ids[:, None]
    slot_length = jnp.sum(jnp.where(matches, lengths[None, :], 0), axis=1)
    owner_of = request_slot // slot_count
    within = request_slot % slot_count
    earlier = (owner_of[None, :] == device_index) & (
        within[None, :] < jnp.arange(slot_count, dtype=jnp.int32)[:, None]
    )
    slot_offset = jnp.sum(jnp.where(earlier, lengths[None, :], 0), axis=1)
    position = slot_length.astype(jnp.float32)[:, None, None]
    query_heads = rotate(rms_scale(query_full, query_gain), position).astype(jnp.bfloat16)
    query_heads = query_heads.reshape(slot_count, kv_count, group_size, head_dim)
    key_new = rotate(rms_scale(key_full, key_gain), position).astype(jnp.bfloat16)
    pool_tokens = key_cache.shape[0]
    cached_keys = key_cache.reshape(pool_tokens, kv_count, head_dim)
    cached_values = value_cache.reshape(pool_tokens, kv_count, head_dim)
    scale_factor = 1.0 / math.sqrt(head_dim)
    scores = (
        jnp.einsum("skgd,tkd->skgt", query_heads, cached_keys, preferred_element_type=jnp.float32)
        * scale_factor
    )
    own_score = (
        jnp.einsum("skgd,skd->skg", query_heads, key_new, preferred_element_type=jnp.float32)
        * scale_factor
    )
    token_pos = jnp.arange(pool_tokens, dtype=jnp.int32)
    inside = (token_pos[None, :] >= slot_offset[:, None]) & (
        token_pos[None, :] < (slot_offset + slot_length)[:, None]
    )
    inside = inside[:, None, None, :]
    largest = jnp.maximum(jnp.max(jnp.where(inside, scores, -1e30), axis=3), own_score)
    weights = jnp.where(inside, jnp.exp(scores - largest[..., None]), 0.0)
    own_weight = jnp.exp(own_score - largest)
    denominator = jnp.sum(weights, axis=3) + own_weight
    summed = jnp.einsum(
        "skgt,tkd->skgd",
        weights.astype(jnp.bfloat16),
        cached_values,
        preferred_element_type=jnp.float32,
    )
    own_low = own_weight.astype(jnp.bfloat16).astype(jnp.float32)
    summed = summed + own_low[..., None] * value_new.astype(jnp.float32)[:, :, None, :]
    head_out = (
        (summed / denominator[..., None])
        .astype(jnp.bfloat16)
        .reshape(slot_count, devices, query_cols)
    )
    returned = lax.all_to_all(head_out, ("pool", "tensor"), split_axis=1, concat_axis=0, tiled=True)
    head_rows = returned.reshape(devices * slot_count, query_cols)[request_slot]
    partial_value = jnp.dot(head_rows, output_weight, preferred_element_type=jnp.float32)
    row_start = device_index * local_rows
    own_part = lax.dynamic_slice_in_dim(partial_value, row_start, local_rows, 0) + hidden.astype(
        jnp.float32
    )
    partial_value = lax.dynamic_update_slice_in_dim(partial_value, own_part, row_start, 0)
    totals = lax.psum(partial_value, ("pool", "tensor"))
    mixed_all = totals.astype(jnp.bfloat16)
    mixed_rows = lax.dynamic_slice_in_dim(mixed_all, row_start, local_rows, 0)
    post_normed = rms_scale(mixed_all, post_gain).astype(jnp.bfloat16)
    gate_part = jnp.dot(post_normed, gate_weight, preferred_element_type=jnp.float32)
    up_part = jnp.dot(post_normed, up_weight, preferred_element_type=jnp.float32)
    activated = (jax.nn.silu(gate_part) * up_part).astype(jnp.bfloat16)
    lowered = lax.psum_scatter(
        jnp.dot(activated, down_weight, preferred_element_type=jnp.float32),
        ("pool", "tensor"),
        scatter_dimension=0,
        tiled=True,
    )
    final_rows = (mixed_rows.astype(jnp.float32) + lowered).astype(jnp.bfloat16)
    return (mixed_rows, final_rows)


MESH = pl.DeviceIdType.MESH
F32 = jnp.float32
BF16 = jnp.bfloat16


def step_kernel(
    pool,
    tensor,
    hidden_ref,
    input_gain_ref,
    query_gain_ref,
    key_gain_ref,
    post_gain_ref,
    length_ref,
    slot_ref,
    frequency_ref,
    qw_hbm,
    kw_hbm,
    vw_hbm,
    ow_hbm,
    gw_hbm,
    uw_hbm,
    dw_hbm,
    kc_hbm,
    vc_hbm,
    mixed_ref,
    final_ref,
    qw,
    kw,
    vw,
    ow,
    gw,
    uw,
    dw,
    kc,
    vc,
    ag1,
    ag2,
    xs,
    slots,
    to_owner,
    at_owner,
    qs,
    kvs,
    ho,
    to_home,
    at_home,
    back,
    part1,
    peer1,
    out1,
    in1,
    part2,
    peer2,
    out2,
    in2,
    load_sem,
    ag1_s,
    ag1_r,
    ag2_s,
    ag2_r,
    a1_s,
    a1_r,
    a2_s,
    a2_r,
    rs1_s,
    rs1_r,
    rs2_s,
    rs2_r,
):
    devices = pool * tensor
    rows, width = hidden_ref.shape
    requests = devices * rows
    head_dim = query_gain_ref.shape[1]
    query_cols = qw.shape[1]
    key_cols = kw.shape[1]
    heads_here = query_cols // head_dim
    head_count = devices * heads_here
    kv_count = devices * key_cols // head_dim
    per_kv = devices // kv_count
    group = head_count // kv_count
    hidden_units = gw.shape[1]
    p = lax.axis_index("pool")
    t = lax.axis_index("tensor")
    me = p * tensor + t
    partner = {"pool": 1 - p, "tensor": t}

    loads = [
        pltpu.make_async_copy(a, b, load_sem.at[i])
        for i, (a, b) in enumerate(
            [
                (qw_hbm, qw),
                (kw_hbm, kw),
                (vw_hbm, vw),
                (kc_hbm, kc),
                (vc_hbm, vc),
                (ow_hbm, ow),
                (gw_hbm, gw),
                (uw_hbm, uw),
                (dw_hbm, dw),
            ]
        )
    ]
    for load in loads:
        load.start()

    def place(index):
        return {"pool": lax.div(index, tensor), "tensor": lax.rem(index, tensor)}

    def each(first, last, body):
        def run(j, carry):
            body(j)
            return carry

        lax.fori_loop(first, last, run, 0)

    barrier = pltpu.get_barrier_semaphore()
    each(
        1,
        devices,
        lambda j: pl.semaphore_signal(
            barrier, inc=1, device_id=place(lax.rem(me + j, devices)), device_id_type=MESH
        ),
    )

    def remote(source, target, sent, received, where):
        return pltpu.make_async_remote_copy(
            src_ref=source,
            dst_ref=target,
            send_sem=sent,
            recv_sem=received,
            device_id=where,
            device_id_type=MESH,
        )

    def gather(buffer, sent, received):
        def peer_copy(j):
            return remote(
                buffer.at[me],
                buffer.at[me],
                sent.at[j],
                received.at[me],
                {"pool": p, "tensor": lax.rem(t + j, tensor)},
            )

        own_copy = remote(buffer.at[me], buffer.at[me], sent.at[0], received.at[me], partner)

        def passed(j):
            index = p * tensor + lax.rem(t + j, tensor)
            return remote(
                buffer.at[index],
                buffer.at[index],
                sent.at[tensor + j],
                received.at[index],
                partner,
            )

        def from_partner(j):
            index = (1 - p) * tensor + lax.rem(t + j, tensor)
            return remote(
                buffer.at[index], buffer.at[index], sent.at[0], received.at[index], partner
            )

        each(1, tensor, lambda j: peer_copy(j).start())
        own_copy.start()

        def forward(j):
            passed(j).wait_recv()
            passed(j).start()

        each(1, tensor, forward)
        each(0, tensor, lambda j: from_partner(j).wait_recv())

        def finish():
            own_copy.wait_send()
            each(1, tensor, lambda j: peer_copy(j).wait_send())
            each(1, tensor, lambda j: passed(j).wait_send())

        return finish

    def exchange(outgoing, incoming, sent, received):
        def copy(j):
            peer = lax.rem(me + j, devices)
            return remote(
                outgoing.at[peer], incoming.at[me], sent.at[j], received.at[me], place(peer)
            )

        def arrival(j):
            peer = lax.rem(me + j, devices)
            return remote(
                outgoing.at[peer], incoming.at[peer], sent.at[j], received.at[peer], place(peer)
            )

        each(1, devices, lambda j: copy(j).start())
        incoming[me] = outgoing[me]
        each(1, devices, lambda j: arrival(j).wait_recv())
        return lambda: each(1, devices, lambda j: copy(j).wait_send())

    def scatter_sum(part, peer, outgoing, incoming, sent, received):
        swap = remote(part.at[1 - p], peer, sent.at[0], received.at[tensor], partner)
        swap.start()
        swap.wait_recv()
        peer[...] = peer[...] + part[p]
        for index in range(tensor):
            outgoing[index] = peer[index * rows : (index + 1) * rows, :].astype(BF16)

        def copy(j):
            other = lax.rem(t + j, tensor)
            return remote(
                outgoing.at[other],
                incoming.at[t],
                sent.at[j],
                received.at[t],
                {"pool": p, "tensor": other},
            )

        def arrival(j):
            other = lax.rem(t + j, tensor)
            return remote(
                outgoing.at[other],
                incoming.at[other],
                sent.at[j],
                received.at[other],
                {"pool": p, "tensor": other},
            )

        each(1, tensor, lambda j: copy(j).start())
        incoming[t] = outgoing[t]
        each(1, tensor, lambda j: arrival(j).wait_recv())
        total = incoming[0].astype(F32)
        for index in range(1, tensor):
            total = total + incoming[index].astype(F32)

        def finish():
            swap.wait_send()
            each(1, tensor, lambda j: copy(j).wait_send())

        return total, finish

    def spread(buffer):
        for index in range(devices):
            xs[index * rows : (index + 1) * rows, :] = buffer[index].astype(F32)

    hidden = hidden_ref[...].astype(F32)
    ag1[me] = rms_scale(hidden, input_gain_ref[...]).astype(BF16)

    slot_row = slot_ref[...]
    length_row = length_ref[...]
    wide = devices * SLOTS
    scatter_hot = (
        lax.broadcasted_iota(jnp.int32, (wide, requests), 0) == slot_row
    ).astype(F32).astype(BF16)
    eye = lax.broadcasted_iota(jnp.int32, (requests, requests), 0) == lax.broadcasted_iota(
        jnp.int32, (requests, requests), 1
    )
    slot_col = jnp.sum(
        jnp.where(eye, jnp.broadcast_to(slot_row, (requests, requests)), 0).astype(F32),
        axis=1,
        keepdims=True,
    ).astype(jnp.int32)
    gather_hot = (
        lax.broadcasted_iota(jnp.int32, (requests, wide), 1) == slot_col
    ).astype(F32).astype(BF16)
    span = 2 * SLOTS
    place_id = lax.rem(lax.broadcasted_iota(jnp.int32, (span, requests), 0), SLOTS)
    slot_wide = jnp.broadcast_to(slot_row, (span, requests))
    length_wide = jnp.broadcast_to(length_row, (span, requests)).astype(F32)
    base = me * SLOTS
    slot_length = jnp.sum(
        jnp.where(slot_wide == base + place_id, length_wide, 0.0), axis=1, keepdims=True
    )
    slot_offset = jnp.sum(
        jnp.where((slot_wide >= base) & (slot_wide < base + place_id), length_wide, 0.0),
        axis=1,
        keepdims=True,
    )
    angles = slot_length * frequency_ref[...]
    cosine = jnp.cos(angles)
    lane = lax.broadcasted_iota(jnp.int32, (span, head_dim), 1)
    sine_part = jnp.where(lane < head_dim // 2, -jnp.sin(angles), jnp.sin(angles))
    pool_tokens = kc.shape[0]
    token = lax.broadcasted_iota(jnp.int32, (span, pool_tokens), 1).astype(F32)
    inside = jnp.where(
        (token >= slot_offset) & (token < slot_offset + slot_length), 1.0, 0.0
    )

    def turn(values, scale, copies):
        scaled = rms_scale(values, scale)
        return scaled * jnp.tile(cosine, (copies, 1)) + pltpu.roll(
            scaled, head_dim // 2, 1
        ) * jnp.tile(sine_part, (copies, 1))

    pl.semaphore_wait(barrier, devices - 1)
    done = [gather(ag1, ag1_s, ag1_r)]
    spread(ag1)
    for load in loads[:3]:
        load.wait()
    chunk = math.gcd(width, 512)

    def project(i, carry):
        at = pl.ds(pl.multiple_of(i * chunk, chunk), chunk)
        left = xs[:, at].astype(BF16)
        return tuple(
            acc + jnp.dot(left, w[at, :], preferred_element_type=F32)
            for acc, w in zip(carry, (qw, kw, vw))
        )

    query_part, key_part, value_part = lax.fori_loop(
        0,
        width // chunk,
        project,
        (
            jnp.zeros((requests, query_cols), F32),
            jnp.zeros((requests, key_cols), F32),
            jnp.zeros((requests, key_cols), F32),
        ),
    )

    def shift(count, amount):
        low = lax.broadcasted_iota(jnp.int32, (count, head_dim), 0)
        high = lax.broadcasted_iota(jnp.int32, (count, head_dim), 1)
        return (low + amount == high).astype(F32).astype(BF16)

    kv_part = jnp.dot(
        key_part.astype(BF16), shift(key_cols, 0), preferred_element_type=F32
    ) + jnp.dot(value_part.astype(BF16), shift(key_cols, key_cols), preferred_element_type=F32)
    slots[:, :query_cols] = jnp.dot(
        scatter_hot, query_part.astype(BF16), preferred_element_type=F32
    )
    slots[:, query_cols:] = jnp.dot(
        scatter_hot, kv_part.astype(BF16), preferred_element_type=F32
    )
    for index in range(devices):
        to_owner[index] = slots[index * SLOTS : (index + 1) * SLOTS, :].astype(BF16)
    done.append(exchange(to_owner, at_owner, a1_s, a1_r))

    for index in range(devices):
        arrived = at_owner[index].astype(F32)
        for j in range(heads_here):
            at = (index * heads_here + j) * SLOTS
            qs[at : at + SLOTS, :] = arrived[:, j * head_dim : (j + 1) * head_dim]
        at = (index // per_kv) * span
        lanes = (index % per_kv) * head_dim
        kvs[at : at + SLOTS, lanes : lanes + head_dim] = arrived[:, query_cols:]
        kvs[at + SLOTS : at + span, lanes : lanes + head_dim] = arrived[:, query_cols:]

    low = lax.broadcasted_iota(jnp.int32, (per_kv * head_dim, head_dim), 0)
    high = lax.broadcasted_iota(jnp.int32, (per_kv * head_dim, head_dim), 1)
    piece = lax.div(low, head_dim)
    inner = lax.rem(low, head_dim)
    key_hot = ((inner < key_cols) & (piece * key_cols + inner == high)).astype(F32).astype(BF16)
    value_hot = (
        ((inner >= key_cols) & (inner < 2 * key_cols) & (piece * key_cols + inner - key_cols == high))
        .astype(F32)
        .astype(BF16)
    )
    pieces = kvs[...].astype(BF16)
    key_new = turn(
        jnp.dot(pieces, key_hot, preferred_element_type=F32), key_gain_ref[...], kv_count
    ).astype(BF16)
    value_new = jnp.dot(pieces, value_hot, preferred_element_type=F32)
    scale_factor = 1.0 / math.sqrt(head_dim)
    block = group * SLOTS
    copies = block // span
    allowed = jnp.tile(inside, (copies, 1)) > 0.5
    for load in loads[3:5]:
        load.wait()
    for k in range(kv_count):
        query = turn(qs[k * block : (k + 1) * block, :], query_gain_ref[...], copies).astype(BF16)
        lanes = slice(k * head_dim, (k + 1) * head_dim)
        scores = (
            lax.dot_general(
                query, kc[:, lanes], (((1,), (1,)), ((), ())), preferred_element_type=F32
            )
            * scale_factor
        )
        own_key = jnp.tile(key_new[k * span : (k + 1) * span, :].astype(F32), (copies, 1))
        own_value = jnp.tile(value_new[k * span : (k + 1) * span, :], (copies, 1))
        own_score = jnp.sum(query.astype(F32) * own_key, axis=1, keepdims=True) * scale_factor
        scores = jnp.where(allowed, scores, -1e30)
        largest = jnp.maximum(jnp.max(scores, axis=1, keepdims=True), own_score)
        weights = jnp.exp(scores - largest)
        own_weight = jnp.exp(own_score - largest)
        denominator = jnp.sum(weights, axis=1, keepdims=True) + own_weight
        summed = jnp.dot(weights.astype(BF16), vc[:, lanes], preferred_element_type=F32)
        summed = summed + own_weight.astype(BF16).astype(F32) * own_value
        ho[k * block : (k + 1) * block, :] = summed / denominator
    for index in range(devices):
        for j in range(heads_here):
            at = (index * heads_here + j) * SLOTS
            to_home[index, :, j * head_dim : (j + 1) * head_dim] = ho[at : at + SLOTS, :].astype(BF16)
    done.append(exchange(to_home, at_home, a2_s, a2_r))
    for index in range(devices):
        back[index * SLOTS : (index + 1) * SLOTS, :] = at_home[index].astype(F32)
    head_rows = jnp.dot(
        gather_hot, back[...].astype(BF16), preferred_element_type=F32
    ).astype(BF16)

    half = tensor * rows

    def multiply(left, weight, part):
        def columns(i):
            at = pl.ds(pl.multiple_of(i * chunk, chunk), chunk)
            product = jnp.dot(left, weight[:, at], preferred_element_type=F32)
            for q in range(pool):
                part[q, :, at] = product[q * half : (q + 1) * half, :]

        each(0, width // chunk, columns)

    loads[5].wait()
    multiply(head_rows, ow, part1)
    total, finish = scatter_sum(part1, peer1, out1, in1, rs1_s, rs1_r)
    done.append(finish)
    mixed = (total + hidden).astype(BF16)
    mixed_ref[...] = mixed
    ag2[me] = rms_scale(mixed, post_gain_ref[...]).astype(BF16)
    done.append(gather(ag2, ag2_s, ag2_r))
    spread(ag2)
    loads[6].wait()
    loads[7].wait()

    def expand(i, carry):
        at = pl.ds(pl.multiple_of(i * chunk, chunk), chunk)
        left = xs[:, at].astype(BF16)
        return tuple(
            acc + jnp.dot(left, w[at, :], preferred_element_type=F32)
            for acc, w in zip(carry, (gw, uw))
        )

    gate_part, up_part = lax.fori_loop(
        0,
        width // chunk,
        expand,
        (jnp.zeros((requests, hidden_units), F32), jnp.zeros((requests, hidden_units), F32)),
    )
    activated = (gate_part / (1.0 + jnp.exp(-gate_part)) * up_part).astype(BF16)
    loads[8].wait()
    multiply(activated, dw, part2)
    total, finish = scatter_sum(part2, peer2, out2, in2, rs2_s, rs2_r)
    done.append(finish)
    final_ref[...] = (mixed_ref[...].astype(F32) + total).astype(BF16)
    for finish in done:
        finish()


def fused(pool, tensor, *operands):
    (
        hidden,
        input_gain,
        query_weight,
        key_weight,
        value_weight,
        query_gain,
        key_gain,
        output_weight,
        post_gain,
        gate_weight,
        up_weight,
        down_weight,
        key_cache,
        value_cache,
        lengths,
        request_slot,
    ) = operands
    devices = pool * tensor
    rows, width = hidden.shape
    head_dim = query_gain.shape[0]
    query_cols = query_weight.shape[1]
    key_cols = key_weight.shape[1]
    heads_here = query_cols // head_dim
    kv_count = devices * key_cols // head_dim
    per_kv = devices // kv_count
    requests = devices * rows
    half_width = head_dim // 2
    frequency = theta ** (-jnp.arange(half_width, dtype=jnp.float32) * 2.0 / head_dim)
    frequency = jnp.concatenate([frequency, frequency])[None, :]
    heavy = (
        query_weight,
        key_weight,
        value_weight,
        output_weight,
        gate_weight,
        up_weight,
        down_weight,
        key_cache,
        value_cache,
    )
    dma = pltpu.SemaphoreType.DMA
    sent_cols = query_cols + head_dim
    sums = [
        pltpu.VMEM((pool, tensor * rows, width), F32),
        pltpu.VMEM((tensor * rows, width), F32),
        pltpu.VMEM((tensor, rows, width), BF16),
        pltpu.VMEM((tensor, rows, width), BF16),
    ]
    scratch = (
        [pltpu.VMEM(w.shape, w.dtype) for w in heavy]
        + [pltpu.VMEM((devices, rows, width), BF16)] * 2
        + [
            pltpu.VMEM((requests, width), F32),
            pltpu.VMEM((devices * SLOTS, sent_cols), F32),
            pltpu.VMEM((devices, SLOTS, sent_cols), BF16),
            pltpu.VMEM((devices, SLOTS, sent_cols), BF16),
            pltpu.VMEM((devices * heads_here * SLOTS, head_dim), F32),
            pltpu.VMEM((kv_count * 2 * SLOTS, per_kv * head_dim), F32),
            pltpu.VMEM((devices * heads_here * SLOTS, head_dim), F32),
            pltpu.VMEM((devices, SLOTS, query_cols), BF16),
            pltpu.VMEM((devices, SLOTS, query_cols), BF16),
            pltpu.VMEM((devices * SLOTS, query_cols), F32),
        ]
        + sums
        + sums
        + [dma((len(heavy),))]
        + [dma((2 * tensor,)), dma((devices,))] * 2
        + [dma((devices,)), dma((devices,))] * 2
        + [dma((tensor,)), dma((tensor + 1,))] * 2
    )
    vmem = pl.BlockSpec(memory_space=pltpu.VMEM)
    hbm = pl.BlockSpec(memory_space=pl.ANY)
    row = jax.ShapeDtypeStruct(hidden.shape, hidden.dtype)
    return pl.pallas_call(
        functools.partial(step_kernel, pool, tensor),
        out_shape=(row, row),
        in_specs=[vmem] * 8 + [hbm] * len(heavy),
        out_specs=(vmem, vmem),
        scratch_shapes=scratch,
        compiler_params=pltpu.CompilerParams(
            collective_id=0, has_side_effects=True, vmem_limit_bytes=62 * 1024 * 1024
        ),
    )(
        hidden,
        input_gain[None, :],
        query_gain[None, :],
        key_gain[None, :],
        post_gain[None, :],
        lengths[None, :],
        request_slot[None, :],
        frequency,
        *heavy,
    )


def dispatch(pool, tensor, *operands):
    query_cols = operands[2].shape[1]
    key_cols = operands[3].shape[1]
    head_dim = operands[5].shape[0]
    whole_heads = query_cols % head_dim == 0 and head_dim % key_cols == 0
    if pool == 2 and whole_heads and 2 * key_cols <= head_dim:
        return fused(pool, tensor, *operands)
    return on_device(*operands)


def solution(mesh):
    placed = (
        P(("groups", "pool", "tensor"), None),
        P(),
        P(None, ("pool", "tensor")),
        P(None, ("pool", "tensor")),
        P(None, ("pool", "tensor")),
        P(),
        P(),
        P(("pool", "tensor"), None),
        P(),
        P(None, ("pool", "tensor")),
        P(None, ("pool", "tensor")),
        P(("pool", "tensor"), None),
        P(("groups", "pool", "tensor"), None),
        P(("groups", "pool", "tensor"), None),
        P("groups"),
        P("groups"),
    )
    return jax.shard_map(
        functools.partial(dispatch, mesh.shape["pool"], mesh.shape["tensor"]),
        mesh=mesh,
        in_specs=placed,
        out_specs=(P(("groups", "pool", "tensor"), None), P(("groups", "pool", "tensor"), None)),
        check_vma=False,
    )
```

```python
import functools
import math

import jax
import jax.numpy as jnp
import numpy as np
from jax import lax
from jax.experimental import pallas as pl
from jax.experimental.pallas import tpu as pltpu
from jax.sharding import PartitionSpec as P

SLOTS = 4


eps = 1e-06
theta = 1000000.0


def rms_scale(values, scales):
    values = values.astype(jnp.float32)
    return values * lax.rsqrt(jnp.mean(values * values, axis=-1, keepdims=True) + eps) * scales


def rotate(values, position):
    half_width = values.shape[-1] // 2
    frequency = theta ** (-jnp.arange(half_width, dtype=jnp.float32) * 2.0 / values.shape[-1])
    angles = position * frequency
    cosine = jnp.cos(angles)
    sine_part = jnp.sin(angles)
    front_half = values[..., :half_width]
    back_half = values[..., half_width:]
    return jnp.concatenate(
        [front_half * cosine - back_half * sine_part, back_half * cosine + front_half * sine_part],
        axis=-1,
    )


def on_device(
    hidden,
    input_gain,
    query_weight,
    key_weight,
    value_weight,
    query_gain,
    key_gain,
    output_weight,
    post_gain,
    gate_weight,
    up_weight,
    down_weight,
    key_cache,
    value_cache,
    lengths,
    request_slot,
):
    devices = lax.axis_size(("pool", "tensor"))
    device_index = lax.axis_index(("pool", "tensor"))
    local_rows = hidden.shape[0]
    query_cols = query_weight.shape[1]
    key_cols = key_weight.shape[1]
    width_sent = query_cols + 2 * key_cols
    head_dim = query_gain.shape[0]
    slot_count = SLOTS
    head_count = devices * query_cols // head_dim
    kv_count = devices * key_cols // head_dim
    group_size = head_count // kv_count
    normed = rms_scale(hidden, input_gain).astype(jnp.bfloat16)
    shard_rows = lax.all_gather(normed, ("pool", "tensor"), axis=0, tiled=True)
    query_part = jnp.dot(shard_rows, query_weight, preferred_element_type=jnp.float32)
    key_part = jnp.dot(shard_rows, key_weight, preferred_element_type=jnp.float32)
    value_part = jnp.dot(shard_rows, value_weight, preferred_element_type=jnp.float32)
    projected = jnp.concatenate([query_part, key_part, value_part], axis=1).astype(jnp.bfloat16)
    outgoing = (
        jnp.zeros((devices * slot_count, width_sent), jnp.bfloat16).at[request_slot].set(projected)
    )
    outgoing = outgoing.reshape(devices, slot_count, width_sent)
    arrived = lax.all_to_all(
        outgoing, ("pool", "tensor"), split_axis=0, concat_axis=2, tiled=True
    ).reshape(slot_count, devices, width_sent)
    query_full = arrived[:, :, :query_cols].reshape(slot_count, head_count, head_dim)
    key_full = arrived[:, :, query_cols : query_cols + key_cols].reshape(
        slot_count, kv_count, head_dim
    )
    value_new = arrived[:, :, query_cols + key_cols :].reshape(slot_count, kv_count, head_dim)
    slot_ids = device_index * slot_count + jnp.arange(slot_count, dtype=jnp.int32)
    matches = request_slot[None, :] == slot_ids[:, None]
    slot_length = jnp.sum(jnp.where(matches, lengths[None, :], 0), axis=1)
    owner_of = request_slot // slot_count
    within = request_slot % slot_count
    earlier = (owner_of[None, :] == device_index) & (
        within[None, :] < jnp.arange(slot_count, dtype=jnp.int32)[:, None]
    )
    slot_offset = jnp.sum(jnp.where(earlier, lengths[None, :], 0), axis=1)
    position = slot_length.astype(jnp.float32)[:, None, None]
    query_heads = rotate(rms_scale(query_full, query_gain), position).astype(jnp.bfloat16)
    query_heads = query_heads.reshape(slot_count, kv_count, group_size, head_dim)
    key_new = rotate(rms_scale(key_full, key_gain), position).astype(jnp.bfloat16)
    pool_tokens = key_cache.shape[0]
    cached_keys = key_cache.reshape(pool_tokens, kv_count, head_dim)
    cached_values = value_cache.reshape(pool_tokens, kv_count, head_dim)
    scale_factor = 1.0 / math.sqrt(head_dim)
    scores = (
        jnp.einsum("skgd,tkd->skgt", query_heads, cached_keys, preferred_element_type=jnp.float32)
        * scale_factor
    )
    own_score = (
        jnp.einsum("skgd,skd->skg", query_heads, key_new, preferred_element_type=jnp.float32)
        * scale_factor
    )
    token_pos = jnp.arange(pool_tokens, dtype=jnp.int32)
    inside = (token_pos[None, :] >= slot_offset[:, None]) & (
        token_pos[None, :] < (slot_offset + slot_length)[:, None]
    )
    inside = inside[:, None, None, :]
    largest = jnp.maximum(jnp.max(jnp.where(inside, scores, -1e30), axis=3), own_score)
    weights = jnp.where(inside, jnp.exp(scores - largest[..., None]), 0.0)
    own_weight = jnp.exp(own_score - largest)
    denominator = jnp.sum(weights, axis=3) + own_weight
    summed = jnp.einsum(
        "skgt,tkd->skgd",
        weights.astype(jnp.bfloat16),
        cached_values,
        preferred_element_type=jnp.float32,
    )
    own_low = own_weight.astype(jnp.bfloat16).astype(jnp.float32)
    summed = summed + own_low[..., None] * value_new.astype(jnp.float32)[:, :, None, :]
    head_out = (
        (summed / denominator[..., None])
        .astype(jnp.bfloat16)
        .reshape(slot_count, devices, query_cols)
    )
    returned = lax.all_to_all(head_out, ("pool", "tensor"), split_axis=1, concat_axis=0, tiled=True)
    head_rows = returned.reshape(devices * slot_count, query_cols)[request_slot]
    partial_value = jnp.dot(head_rows, output_weight, preferred_element_type=jnp.float32)
    row_start = device_index * local_rows
    own_part = lax.dynamic_slice_in_dim(partial_value, row_start, local_rows, 0) + hidden.astype(
        jnp.float32
    )
    partial_value = lax.dynamic_update_slice_in_dim(partial_value, own_part, row_start, 0)
    totals = lax.psum(partial_value, ("pool", "tensor"))
    mixed_all = totals.astype(jnp.bfloat16)
    mixed_rows = lax.dynamic_slice_in_dim(mixed_all, row_start, local_rows, 0)
    post_normed = rms_scale(mixed_all, post_gain).astype(jnp.bfloat16)
    gate_part = jnp.dot(post_normed, gate_weight, preferred_element_type=jnp.float32)
    up_part = jnp.dot(post_normed, up_weight, preferred_element_type=jnp.float32)
    activated = (jax.nn.silu(gate_part) * up_part).astype(jnp.bfloat16)
    lowered = lax.psum_scatter(
        jnp.dot(activated, down_weight, preferred_element_type=jnp.float32),
        ("pool", "tensor"),
        scatter_dimension=0,
        tiled=True,
    )
    final_rows = (mixed_rows.astype(jnp.float32) + lowered).astype(jnp.bfloat16)
    return (mixed_rows, final_rows)


MESH = pl.DeviceIdType.MESH
F32 = jnp.float32
BF16 = jnp.bfloat16


def step_kernel(
    pool,
    tensor,
    hidden_ref,
    input_gain_ref,
    query_gain_ref,
    key_gain_ref,
    post_gain_ref,
    length_ref,
    slot_ref,
    frequency_ref,
    qw_hbm,
    kw_hbm,
    vw_hbm,
    ow_hbm,
    gw_hbm,
    uw_hbm,
    dw_hbm,
    kc_hbm,
    vc_hbm,
    mixed_ref,
    final_ref,
    qw,
    kw,
    vw,
    ow,
    gw,
    uw,
    dw,
    kc,
    vc,
    ag1,
    ag2,
    xs,
    slots,
    to_owner,
    at_owner,
    qs,
    kvs,
    ho,
    to_home,
    at_home,
    back,
    part1,
    peer1,
    out1,
    in1,
    part2,
    peer2,
    out2,
    in2,
    load_sem,
    ag1_s,
    ag1_r,
    ag2_s,
    ag2_r,
    a1_s,
    a1_r,
    a2_s,
    a2_r,
    rs1_s,
    rs1_r,
    rs2_s,
    rs2_r,
):
    devices = pool * tensor
    rows, width = hidden_ref.shape
    requests = devices * rows
    head_dim = query_gain_ref.shape[1]
    query_cols = qw.shape[1]
    key_cols = kw.shape[0]
    heads_here = query_cols // head_dim
    head_count = devices * heads_here
    kv_count = devices * key_cols // head_dim
    per_kv = devices // kv_count
    group = head_count // kv_count
    hidden_units = gw.shape[0]
    p = lax.axis_index("pool")
    t = lax.axis_index("tensor")
    me = p * tensor + t
    partner = {"pool": 1 - p, "tensor": t}

    loads = [
        pltpu.make_async_copy(a, b, load_sem.at[i])
        for i, (a, b) in enumerate(
            [
                (qw_hbm, qw),
                (kw_hbm, kw),
                (vw_hbm, vw),
                (kc_hbm, kc),
                (vc_hbm, vc),
                (ow_hbm, ow),
                (gw_hbm, gw),
                (uw_hbm, uw),
                (dw_hbm, dw),
            ]
        )
    ]
    for load in loads:
        load.start()

    def place(index):
        return {"pool": lax.div(index, tensor), "tensor": lax.rem(index, tensor)}

    def each(first, last, body):
        def run(j, carry):
            body(j)
            return carry

        lax.fori_loop(first, last, run, 0)

    barrier = pltpu.get_barrier_semaphore()
    each(
        1,
        devices,
        lambda j: pl.semaphore_signal(
            barrier, inc=1, device_id=place(lax.rem(me + j, devices)), device_id_type=MESH
        ),
    )

    def remote(source, target, sent, received, where):
        return pltpu.make_async_remote_copy(
            src_ref=source,
            dst_ref=target,
            send_sem=sent,
            recv_sem=received,
            device_id=where,
            device_id_type=MESH,
        )

    def gather(buffer, sent, received):
        def peer_copy(j):
            return remote(
                buffer.at[me],
                buffer.at[me],
                sent.at[j],
                received.at[me],
                {"pool": p, "tensor": lax.rem(t + j, tensor)},
            )

        own_copy = remote(buffer.at[me], buffer.at[me], sent.at[0], received.at[me], partner)

        def passed(j):
            index = p * tensor + lax.rem(t + j, tensor)
            return remote(
                buffer.at[index],
                buffer.at[index],
                sent.at[tensor + j],
                received.at[index],
                partner,
            )

        def from_partner(j):
            index = (1 - p) * tensor + lax.rem(t + j, tensor)
            return remote(
                buffer.at[index], buffer.at[index], sent.at[0], received.at[index], partner
            )

        each(1, tensor, lambda j: peer_copy(j).start())
        own_copy.start()

        def forward(j):
            passed(j).wait_recv()
            passed(j).start()

        each(1, tensor, forward)
        each(0, tensor, lambda j: from_partner(j).wait_recv())

        def finish():
            own_copy.wait_send()
            each(1, tensor, lambda j: peer_copy(j).wait_send())
            each(1, tensor, lambda j: passed(j).wait_send())

        return finish

    def exchange(outgoing, incoming, sent, received):
        def copy(j):
            peer = lax.rem(me + j, devices)
            return remote(
                outgoing.at[peer], incoming.at[me], sent.at[j], received.at[me], place(peer)
            )

        def arrival(j):
            peer = lax.rem(me + j, devices)
            return remote(
                outgoing.at[peer], incoming.at[peer], sent.at[j], received.at[peer], place(peer)
            )

        each(1, devices, lambda j: copy(j).start())
        incoming[me] = outgoing[me]
        each(1, devices, lambda j: arrival(j).wait_recv())
        return lambda: each(1, devices, lambda j: copy(j).wait_send())

    def scatter_sum(part, peer, outgoing, incoming, sent, received):
        swap = remote(part.at[1 - p], peer, sent.at[0], received.at[tensor], partner)
        swap.start()
        swap.wait_recv()
        peer[...] = peer[...] + part[p]
        for index in range(tensor):
            outgoing[index] = peer[index * rows : (index + 1) * rows, :].astype(BF16)

        def copy(j):
            other = lax.rem(t + j, tensor)
            return remote(
                outgoing.at[other],
                incoming.at[t],
                sent.at[j],
                received.at[t],
                {"pool": p, "tensor": other},
            )

        def arrival(j):
            other = lax.rem(t + j, tensor)
            return remote(
                outgoing.at[other],
                incoming.at[other],
                sent.at[j],
                received.at[other],
                {"pool": p, "tensor": other},
            )

        each(1, tensor, lambda j: copy(j).start())
        incoming[t] = outgoing[t]
        each(1, tensor, lambda j: arrival(j).wait_recv())
        total = incoming[0].astype(F32)
        for index in range(1, tensor):
            total = total + incoming[index].astype(F32)

        def finish():
            swap.wait_send()
            each(1, tensor, lambda j: copy(j).wait_send())

        return total, finish

    def spread(buffer):
        for index in range(devices):
            xs[index * rows : (index + 1) * rows, :] = buffer[index].astype(F32)

    hidden = hidden_ref[...].astype(F32)
    ag1[me] = rms_scale(hidden, input_gain_ref[...]).astype(BF16)

    slot_row = slot_ref[...]
    length_row = length_ref[...]
    wide = devices * SLOTS
    scatter_hot = (
        lax.broadcasted_iota(jnp.int32, (wide, requests), 0) == slot_row
    ).astype(F32).astype(BF16)
    eye = lax.broadcasted_iota(jnp.int32, (requests, requests), 0) == lax.broadcasted_iota(
        jnp.int32, (requests, requests), 1
    )
    slot_col = jnp.sum(
        jnp.where(eye, jnp.broadcast_to(slot_row, (requests, requests)), 0).astype(F32),
        axis=1,
        keepdims=True,
    ).astype(jnp.int32)
    gather_hot = (
        lax.broadcasted_iota(jnp.int32, (requests, wide), 1) == slot_col
    ).astype(F32).astype(BF16)
    span = 2 * SLOTS
    place_id = lax.rem(lax.broadcasted_iota(jnp.int32, (span, requests), 0), SLOTS)
    slot_wide = jnp.broadcast_to(slot_row, (span, requests))
    length_wide = jnp.broadcast_to(length_row, (span, requests)).astype(F32)
    base = me * SLOTS
    slot_length = jnp.sum(
        jnp.where(slot_wide == base + place_id, length_wide, 0.0), axis=1, keepdims=True
    )
    slot_offset = jnp.sum(
        jnp.where((slot_wide >= base) & (slot_wide < base + place_id), length_wide, 0.0),
        axis=1,
        keepdims=True,
    )
    angles = slot_length * frequency_ref[...]
    cosine = jnp.cos(angles)
    lane = lax.broadcasted_iota(jnp.int32, (span, head_dim), 1)
    sine_part = jnp.where(lane < head_dim // 2, -jnp.sin(angles), jnp.sin(angles))
    pool_tokens = kc.shape[0]
    token = lax.broadcasted_iota(jnp.int32, (span, pool_tokens), 1).astype(F32)
    inside = jnp.where(
        (token >= slot_offset) & (token < slot_offset + slot_length), 1.0, 0.0
    )

    def turn(values, scale, copies):
        scaled = rms_scale(values, scale)
        return scaled * jnp.tile(cosine, (copies, 1)) + pltpu.roll(
            scaled, head_dim // 2, 1
        ) * jnp.tile(sine_part, (copies, 1))

    pl.semaphore_wait(barrier, devices - 1)
    done = [gather(ag1, ag1_s, ag1_r)]
    spread(ag1)
    for load in loads[:3]:
        load.wait()
    chunk = math.gcd(width, 512)

    def turned(left, weight, at):
        return lax.dot_general(
            left, weight[:, at], (((1,), (1,)), ((), ())), preferred_element_type=F32
        )

    def project(i, carry):
        at = pl.ds(pl.multiple_of(i * chunk, chunk), chunk)
        left = xs[:, at].astype(BF16)
        return tuple(
            acc + product
            for acc, product in zip(
                carry,
                (
                    jnp.dot(left, qw[at, :], preferred_element_type=F32),
                    turned(left, kw, at),
                    turned(left, vw, at),
                ),
            )
        )

    query_part, key_part, value_part = lax.fori_loop(
        0,
        width // chunk,
        project,
        (
            jnp.zeros((requests, query_cols), F32),
            jnp.zeros((requests, key_cols), F32),
            jnp.zeros((requests, key_cols), F32),
        ),
    )

    def shift(count, amount):
        low = lax.broadcasted_iota(jnp.int32, (count, head_dim), 0)
        high = lax.broadcasted_iota(jnp.int32, (count, head_dim), 1)
        return (low + amount == high).astype(F32).astype(BF16)

    kv_part = jnp.dot(
        key_part.astype(BF16), shift(key_cols, 0), preferred_element_type=F32
    ) + jnp.dot(value_part.astype(BF16), shift(key_cols, key_cols), preferred_element_type=F32)
    slots[:, :query_cols] = jnp.dot(
        scatter_hot, query_part.astype(BF16), preferred_element_type=F32
    )
    slots[:, query_cols:] = jnp.dot(
        scatter_hot, kv_part.astype(BF16), preferred_element_type=F32
    )
    for index in range(devices):
        to_owner[index] = slots[index * SLOTS : (index + 1) * SLOTS, :].astype(BF16)
    done.append(exchange(to_owner, at_owner, a1_s, a1_r))

    for index in range(devices):
        arrived = at_owner[index].astype(F32)
        for j in range(heads_here):
            at = (index * heads_here + j) * SLOTS
            qs[at : at + SLOTS, :] = arrived[:, j * head_dim : (j + 1) * head_dim]
        at = (index // per_kv) * span
        lanes = (index % per_kv) * head_dim
        kvs[at : at + SLOTS, lanes : lanes + head_dim] = arrived[:, query_cols:]
        kvs[at + SLOTS : at + span, lanes : lanes + head_dim] = arrived[:, query_cols:]

    low = lax.broadcasted_iota(jnp.int32, (per_kv * head_dim, head_dim), 0)
    high = lax.broadcasted_iota(jnp.int32, (per_kv * head_dim, head_dim), 1)
    piece = lax.div(low, head_dim)
    inner = lax.rem(low, head_dim)
    key_hot = ((inner < key_cols) & (piece * key_cols + inner == high)).astype(F32).astype(BF16)
    value_hot = (
        ((inner >= key_cols) & (inner < 2 * key_cols) & (piece * key_cols + inner - key_cols == high))
        .astype(F32)
        .astype(BF16)
    )
    pieces = kvs[...].astype(BF16)
    key_new = turn(
        jnp.dot(pieces, key_hot, preferred_element_type=F32), key_gain_ref[...], kv_count
    ).astype(BF16)
    value_new = jnp.dot(pieces, value_hot, preferred_element_type=F32)
    scale_factor = 1.0 / math.sqrt(head_dim)
    block = group * SLOTS
    copies = block // span
    allowed = jnp.tile(inside, (copies, 1)) > 0.5
    for load in loads[3:5]:
        load.wait()
    for k in range(kv_count):
        query = turn(qs[k * block : (k + 1) * block, :], query_gain_ref[...], copies).astype(BF16)
        lanes = slice(k * head_dim, (k + 1) * head_dim)
        scores = (
            lax.dot_general(
                query, kc[:, lanes], (((1,), (1,)), ((), ())), preferred_element_type=F32
            )
            * scale_factor
        )
        own_key = jnp.tile(key_new[k * span : (k + 1) * span, :].astype(F32), (copies, 1))
        own_value = jnp.tile(value_new[k * span : (k + 1) * span, :], (copies, 1))
        own_score = jnp.sum(query.astype(F32) * own_key, axis=1, keepdims=True) * scale_factor
        scores = jnp.where(allowed, scores, -1e30)
        largest = jnp.maximum(jnp.max(scores, axis=1, keepdims=True), own_score)
        weights = jnp.exp(scores - largest)
        own_weight = jnp.exp(own_score - largest)
        denominator = jnp.sum(weights, axis=1, keepdims=True) + own_weight
        summed = jnp.dot(weights.astype(BF16), vc[:, lanes], preferred_element_type=F32)
        summed = summed + own_weight.astype(BF16).astype(F32) * own_value
        ho[k * block : (k + 1) * block, :] = summed / denominator
    for index in range(devices):
        for j in range(heads_here):
            at = (index * heads_here + j) * SLOTS
            to_home[index, :, j * head_dim : (j + 1) * head_dim] = ho[at : at + SLOTS, :].astype(BF16)
    done.append(exchange(to_home, at_home, a2_s, a2_r))
    for index in range(devices):
        back[index * SLOTS : (index + 1) * SLOTS, :] = at_home[index].astype(F32)
    head_rows = jnp.dot(
        gather_hot, back[...].astype(BF16), preferred_element_type=F32
    ).astype(BF16)

    half = tensor * rows

    def multiply(left, weight, part):
        def columns(i):
            at = pl.ds(pl.multiple_of(i * chunk, chunk), chunk)
            product = jnp.dot(left, weight[:, at], preferred_element_type=F32)
            for q in range(pool):
                part[q, :, at] = product[q * half : (q + 1) * half, :]

        each(0, width // chunk, columns)

    loads[5].wait()
    multiply(head_rows, ow, part1)
    total, finish = scatter_sum(part1, peer1, out1, in1, rs1_s, rs1_r)
    done.append(finish)
    mixed = (total + hidden).astype(BF16)
    mixed_ref[...] = mixed
    ag2[me] = rms_scale(mixed, post_gain_ref[...]).astype(BF16)
    done.append(gather(ag2, ag2_s, ag2_r))
    spread(ag2)
    loads[6].wait()
    loads[7].wait()

    def expand(i, carry):
        at = pl.ds(pl.multiple_of(i * chunk, chunk), chunk)
        left = xs[:, at].astype(BF16)
        return tuple(
            acc + turned(left, w, at)
            for acc, w in zip(carry, (gw, uw))
        )

    gate_part, up_part = lax.fori_loop(
        0,
        width // chunk,
        expand,
        (jnp.zeros((requests, hidden_units), F32), jnp.zeros((requests, hidden_units), F32)),
    )
    activated = (gate_part / (1.0 + jnp.exp(-gate_part)) * up_part).astype(BF16)
    loads[8].wait()
    multiply(activated, dw, part2)
    total, finish = scatter_sum(part2, peer2, out2, in2, rs2_s, rs2_r)
    done.append(finish)
    final_ref[...] = (mixed_ref[...].astype(F32) + total).astype(BF16)
    for finish in done:
        finish()


def fused(pool, tensor, *operands):
    (
        hidden,
        input_gain,
        query_weight,
        key_weight,
        value_weight,
        query_gain,
        key_gain,
        output_weight,
        post_gain,
        gate_weight,
        up_weight,
        down_weight,
        key_cache,
        value_cache,
        lengths,
        request_slot,
    ) = operands
    devices = pool * tensor
    rows, width = hidden.shape
    head_dim = query_gain.shape[0]
    query_cols = query_weight.shape[1]
    key_cols = key_weight.shape[1]
    heads_here = query_cols // head_dim
    kv_count = devices * key_cols // head_dim
    per_kv = devices // kv_count
    requests = devices * rows
    half_width = head_dim // 2
    frequency = theta ** (-np.arange(half_width) * 2.0 / head_dim)
    frequency = np.concatenate([frequency, frequency])[None, :].astype(np.float32)
    heavy = (
        query_weight,
        key_weight.T,
        value_weight.T,
        output_weight,
        gate_weight.T,
        up_weight.T,
        down_weight,
        key_cache,
        value_cache,
    )
    dma = pltpu.SemaphoreType.DMA
    sent_cols = query_cols + head_dim
    sums = [
        pltpu.VMEM((pool, tensor * rows, width), F32),
        pltpu.VMEM((tensor * rows, width), F32),
        pltpu.VMEM((tensor, rows, width), BF16),
        pltpu.VMEM((tensor, rows, width), BF16),
    ]
    scratch = (
        [pltpu.VMEM(w.shape, w.dtype) for w in heavy]
        + [pltpu.VMEM((devices, rows, width), BF16)] * 2
        + [
            pltpu.VMEM((requests, width), F32),
            pltpu.VMEM((devices * SLOTS, sent_cols), F32),
            pltpu.VMEM((devices, SLOTS, sent_cols), BF16),
            pltpu.VMEM((devices, SLOTS, sent_cols), BF16),
            pltpu.VMEM((devices * heads_here * SLOTS, head_dim), F32),
            pltpu.VMEM((kv_count * 2 * SLOTS, per_kv * head_dim), F32),
            pltpu.VMEM((devices * heads_here * SLOTS, head_dim), F32),
            pltpu.VMEM((devices, SLOTS, query_cols), BF16),
            pltpu.VMEM((devices, SLOTS, query_cols), BF16),
            pltpu.VMEM((devices * SLOTS, query_cols), F32),
        ]
        + sums
        + sums
        + [dma((len(heavy),))]
        + [dma((2 * tensor,)), dma((devices,))] * 2
        + [dma((devices,)), dma((devices,))] * 2
        + [dma((tensor,)), dma((tensor + 1,))] * 2
    )
    vmem = pl.BlockSpec(memory_space=pltpu.VMEM)
    hbm = pl.BlockSpec(memory_space=pl.ANY)
    row = jax.ShapeDtypeStruct(hidden.shape, hidden.dtype)
    return pl.pallas_call(
        functools.partial(step_kernel, pool, tensor),
        out_shape=(row, row),
        in_specs=[vmem] * 8 + [hbm] * len(heavy),
        out_specs=(vmem, vmem),
        scratch_shapes=scratch,
        compiler_params=pltpu.CompilerParams(
            collective_id=0, has_side_effects=True, vmem_limit_bytes=62 * 1024 * 1024
        ),
    )(
        hidden,
        input_gain[None, :],
        query_gain[None, :],
        key_gain[None, :],
        post_gain[None, :],
        lengths[None, :],
        request_slot[None, :],
        frequency,
        *heavy,
    )


def dispatch(pool, tensor, *operands):
    query_cols = operands[2].shape[1]
    key_cols = operands[3].shape[1]
    head_dim = operands[5].shape[0]
    whole_heads = query_cols % head_dim == 0 and head_dim % key_cols == 0
    if pool == 2 and whole_heads and 2 * key_cols <= head_dim:
        return fused(pool, tensor, *operands)
    return on_device(*operands)


def solution(mesh):
    placed = (
        P(("groups", "pool", "tensor"), None),
        P(),
        P(None, ("pool", "tensor")),
        P(None, ("pool", "tensor")),
        P(None, ("pool", "tensor")),
        P(),
        P(),
        P(("pool", "tensor"), None),
        P(),
        P(None, ("pool", "tensor")),
        P(None, ("pool", "tensor")),
        P(("pool", "tensor"), None),
        P(("groups", "pool", "tensor"), None),
        P(("groups", "pool", "tensor"), None),
        P("groups"),
        P("groups"),
    )
    return jax.shard_map(
        functools.partial(dispatch, mesh.shape["pool"], mesh.shape["tensor"]),
        mesh=mesh,
        in_specs=placed,
        out_specs=(P(("groups", "pool", "tensor"), None), P(("groups", "pool", "tensor"), None)),
        check_vma=False,
    )
```

```python
import functools
import math

import jax
import jax.numpy as jnp
import numpy as np
from jax import lax
from jax.experimental import pallas as pl
from jax.experimental.pallas import tpu as pltpu
from jax.sharding import PartitionSpec as P

SLOTS = 4


eps = 1e-06
theta = 1000000.0


def rms_scale(values, scales):
    values = values.astype(jnp.float32)
    return values * lax.rsqrt(jnp.mean(values * values, axis=-1, keepdims=True) + eps) * scales


def rotate(values, position):
    half_width = values.shape[-1] // 2
    frequency = theta ** (-jnp.arange(half_width, dtype=jnp.float32) * 2.0 / values.shape[-1])
    angles = position * frequency
    cosine = jnp.cos(angles)
    sine_part = jnp.sin(angles)
    front_half = values[..., :half_width]
    back_half = values[..., half_width:]
    return jnp.concatenate(
        [front_half * cosine - back_half * sine_part, back_half * cosine + front_half * sine_part],
        axis=-1,
    )


def on_device(
    hidden,
    input_gain,
    query_weight,
    key_weight,
    value_weight,
    query_gain,
    key_gain,
    output_weight,
    post_gain,
    gate_weight,
    up_weight,
    down_weight,
    key_cache,
    value_cache,
    lengths,
    request_slot,
):
    devices = lax.axis_size(("pool", "tensor"))
    device_index = lax.axis_index(("pool", "tensor"))
    local_rows = hidden.shape[0]
    query_cols = query_weight.shape[1]
    key_cols = key_weight.shape[1]
    width_sent = query_cols + 2 * key_cols
    head_dim = query_gain.shape[0]
    slot_count = SLOTS
    head_count = devices * query_cols // head_dim
    kv_count = devices * key_cols // head_dim
    group_size = head_count // kv_count
    normed = rms_scale(hidden, input_gain).astype(jnp.bfloat16)
    shard_rows = lax.all_gather(normed, ("pool", "tensor"), axis=0, tiled=True)
    query_part = jnp.dot(shard_rows, query_weight, preferred_element_type=jnp.float32)
    key_part = jnp.dot(shard_rows, key_weight, preferred_element_type=jnp.float32)
    value_part = jnp.dot(shard_rows, value_weight, preferred_element_type=jnp.float32)
    projected = jnp.concatenate([query_part, key_part, value_part], axis=1).astype(jnp.bfloat16)
    outgoing = (
        jnp.zeros((devices * slot_count, width_sent), jnp.bfloat16).at[request_slot].set(projected)
    )
    outgoing = outgoing.reshape(devices, slot_count, width_sent)
    arrived = lax.all_to_all(
        outgoing, ("pool", "tensor"), split_axis=0, concat_axis=2, tiled=True
    ).reshape(slot_count, devices, width_sent)
    query_full = arrived[:, :, :query_cols].reshape(slot_count, head_count, head_dim)
    key_full = arrived[:, :, query_cols : query_cols + key_cols].reshape(
        slot_count, kv_count, head_dim
    )
    value_new = arrived[:, :, query_cols + key_cols :].reshape(slot_count, kv_count, head_dim)
    slot_ids = device_index * slot_count + jnp.arange(slot_count, dtype=jnp.int32)
    matches = request_slot[None, :] == slot_ids[:, None]
    slot_length = jnp.sum(jnp.where(matches, lengths[None, :], 0), axis=1)
    owner_of = request_slot // slot_count
    within = request_slot % slot_count
    earlier = (owner_of[None, :] == device_index) & (
        within[None, :] < jnp.arange(slot_count, dtype=jnp.int32)[:, None]
    )
    slot_offset = jnp.sum(jnp.where(earlier, lengths[None, :], 0), axis=1)
    position = slot_length.astype(jnp.float32)[:, None, None]
    query_heads = rotate(rms_scale(query_full, query_gain), position).astype(jnp.bfloat16)
    query_heads = query_heads.reshape(slot_count, kv_count, group_size, head_dim)
    key_new = rotate(rms_scale(key_full, key_gain), position).astype(jnp.bfloat16)
    pool_tokens = key_cache.shape[0]
    cached_keys = key_cache.reshape(pool_tokens, kv_count, head_dim)
    cached_values = value_cache.reshape(pool_tokens, kv_count, head_dim)
    scale_factor = 1.0 / math.sqrt(head_dim)
    scores = (
        jnp.einsum("skgd,tkd->skgt", query_heads, cached_keys, preferred_element_type=jnp.float32)
        * scale_factor
    )
    own_score = (
        jnp.einsum("skgd,skd->skg", query_heads, key_new, preferred_element_type=jnp.float32)
        * scale_factor
    )
    token_pos = jnp.arange(pool_tokens, dtype=jnp.int32)
    inside = (token_pos[None, :] >= slot_offset[:, None]) & (
        token_pos[None, :] < (slot_offset + slot_length)[:, None]
    )
    inside = inside[:, None, None, :]
    largest = jnp.maximum(jnp.max(jnp.where(inside, scores, -1e30), axis=3), own_score)
    weights = jnp.where(inside, jnp.exp(scores - largest[..., None]), 0.0)
    own_weight = jnp.exp(own_score - largest)
    denominator = jnp.sum(weights, axis=3) + own_weight
    summed = jnp.einsum(
        "skgt,tkd->skgd",
        weights.astype(jnp.bfloat16),
        cached_values,
        preferred_element_type=jnp.float32,
    )
    own_low = own_weight.astype(jnp.bfloat16).astype(jnp.float32)
    summed = summed + own_low[..., None] * value_new.astype(jnp.float32)[:, :, None, :]
    head_out = (
        (summed / denominator[..., None])
        .astype(jnp.bfloat16)
        .reshape(slot_count, devices, query_cols)
    )
    returned = lax.all_to_all(head_out, ("pool", "tensor"), split_axis=1, concat_axis=0, tiled=True)
    head_rows = returned.reshape(devices * slot_count, query_cols)[request_slot]
    partial_value = jnp.dot(head_rows, output_weight, preferred_element_type=jnp.float32)
    row_start = device_index * local_rows
    own_part = lax.dynamic_slice_in_dim(partial_value, row_start, local_rows, 0) + hidden.astype(
        jnp.float32
    )
    partial_value = lax.dynamic_update_slice_in_dim(partial_value, own_part, row_start, 0)
    totals = lax.psum(partial_value, ("pool", "tensor"))
    mixed_all = totals.astype(jnp.bfloat16)
    mixed_rows = lax.dynamic_slice_in_dim(mixed_all, row_start, local_rows, 0)
    post_normed = rms_scale(mixed_all, post_gain).astype(jnp.bfloat16)
    gate_part = jnp.dot(post_normed, gate_weight, preferred_element_type=jnp.float32)
    up_part = jnp.dot(post_normed, up_weight, preferred_element_type=jnp.float32)
    activated = (jax.nn.silu(gate_part) * up_part).astype(jnp.bfloat16)
    lowered = lax.psum_scatter(
        jnp.dot(activated, down_weight, preferred_element_type=jnp.float32),
        ("pool", "tensor"),
        scatter_dimension=0,
        tiled=True,
    )
    final_rows = (mixed_rows.astype(jnp.float32) + lowered).astype(jnp.bfloat16)
    return (mixed_rows, final_rows)


MESH = pl.DeviceIdType.MESH
F32 = jnp.float32
SPLIT = 2
BF16 = jnp.bfloat16


def step_kernel(
    pool,
    tensor,
    hidden_ref,
    input_gain_ref,
    query_gain_ref,
    key_gain_ref,
    post_gain_ref,
    length_ref,
    slot_ref,
    frequency_ref,
    qw_hbm,
    kw_hbm,
    vw_hbm,
    ow_hbm,
    gw_hbm,
    uw_hbm,
    dw_hbm,
    kc_hbm,
    vc_hbm,
    both_ref,
    qw,
    kw,
    vw,
    ow,
    gw,
    uw,
    dw,
    kc,
    vc,
    ag1,
    ag2,
    xs,
    slots,
    to_owner,
    at_owner,
    qs,
    kvs,
    ho,
    to_home,
    at_home,
    back,
    part1,
    peer1,
    out1,
    in1,
    part2,
    peer2,
    out2,
    in2,
    load_sem,
    ag1_s,
    ag1_r,
    ag2_s,
    ag2_r,
    a1_s,
    a1_r,
    a2_s,
    a2_r,
    rs1_s,
    rs1_r,
    rs2_s,
    rs2_r,
):
    devices = pool * tensor
    rows, width = hidden_ref.shape
    requests = devices * rows
    head_dim = query_gain_ref.shape[1]
    query_cols = qw.shape[1]
    key_cols = kw.shape[0]
    heads_here = query_cols // head_dim
    head_count = devices * heads_here
    kv_count = devices * key_cols // head_dim
    per_kv = devices // kv_count
    group = head_count // kv_count
    hidden_units = gw.shape[0]
    p = lax.axis_index("pool")
    t = lax.axis_index("tensor")
    me = p * tensor + t
    partner = {"pool": 1 - p, "tensor": t}

    loads = [
        pltpu.make_async_copy(a, b, load_sem.at[i])
        for i, (a, b) in enumerate(
            [
                (qw_hbm, qw),
                (kw_hbm, kw),
                (vw_hbm, vw),
                (kc_hbm, kc),
                (vc_hbm, vc),
                (ow_hbm, ow),
                (gw_hbm, gw),
                (uw_hbm, uw),
                (dw_hbm, dw),
            ]
        )
    ]
    for load in loads:
        load.start()

    def place(index):
        return {"pool": lax.div(index, tensor), "tensor": lax.rem(index, tensor)}

    def each(first, last, body):
        def run(j, carry):
            body(j)
            return carry

        lax.fori_loop(first, last, run, 0)

    barrier = pltpu.get_barrier_semaphore()
    each(
        1,
        devices,
        lambda j: pl.semaphore_signal(
            barrier, inc=1, device_id=place(lax.rem(me + j, devices)), device_id_type=MESH
        ),
    )

    def remote(source, target, sent, received, where):
        return pltpu.make_async_remote_copy(
            src_ref=source,
            dst_ref=target,
            send_sem=sent,
            recv_sem=received,
            device_id=where,
            device_id_type=MESH,
        )

    def gather(buffer, sent, received, lead, advance, carry):
        split = buffer.shape[0]

        def peer_copy(c, j):
            return remote(
                buffer.at[c, me],
                buffer.at[c, me],
                sent.at[c, j],
                received.at[c, me],
                {"pool": p, "tensor": lax.rem(t + j, tensor)},
            )

        def own_copy(c):
            return remote(
                buffer.at[c, me], buffer.at[c, me], sent.at[c, 0], received.at[c, me], partner
            )

        def passed(c, j):
            index = p * tensor + lax.rem(t + j, tensor)
            return remote(
                buffer.at[c, index],
                buffer.at[c, index],
                sent.at[c, tensor + j],
                received.at[c, index],
                partner,
            )

        def from_partner(c, j):
            index = (1 - p) * tensor + lax.rem(t + j, tensor)
            return remote(
                buffer.at[c, index],
                buffer.at[c, index],
                sent.at[c, 0],
                received.at[c, index],
                partner,
            )

        def forward(c, j):
            passed(c, j).wait_recv()
            passed(c, j).start()

        for c in range(split):
            each(1, tensor, lambda j: peer_copy(c, j).start())
            own_copy(c).start()
        each(1, tensor, lambda j: forward(0, j))
        steps = width // split // chunk
        for c in range(split):
            each(0, tensor, lambda j: from_partner(c, j).wait_recv())
            for index in range(devices):
                xs[index * rows : (index + 1) * rows, c * width // split : (c + 1) * width // split] = (
                    buffer[c, index].astype(F32)
                )
            first = c * steps
            if c + 1 < split:
                carry = lax.fori_loop(first, first + lead, advance, carry)
                each(1, tensor, lambda j: forward(c + 1, j))
                first = first + lead
            carry = lax.fori_loop(first, (c + 1) * steps, advance, carry)

        def finish():
            for c in range(split):
                own_copy(c).wait_send()
                each(1, tensor, lambda j: peer_copy(c, j).wait_send())
                each(1, tensor, lambda j: passed(c, j).wait_send())

        return carry, finish

    def exchange(outgoing, incoming, sent, received):
        def copy(j):
            peer = lax.rem(me + j, devices)
            return remote(
                outgoing.at[peer], incoming.at[me], sent.at[j], received.at[me], place(peer)
            )

        def arrival(j):
            peer = lax.rem(me + j, devices)
            return remote(
                outgoing.at[peer], incoming.at[peer], sent.at[j], received.at[peer], place(peer)
            )

        each(1, devices, lambda j: copy(j).start())
        incoming[me] = outgoing[me]
        each(1, devices, lambda j: arrival(j).wait_recv())
        return lambda: each(1, devices, lambda j: copy(j).wait_send())

    def scatter_sum(left, weight, part, peer, outgoing, incoming, sent, received):
        split = part.shape[0]
        wide = width // split

        def swap(c):
            return remote(
                part.at[c, 1 - p], peer.at[c], sent.at[c, 0], received.at[c, tensor], partner
            )

        def copy(c, j):
            other = lax.rem(t + j, tensor)
            return remote(
                outgoing.at[c, other],
                incoming.at[c, t],
                sent.at[c, j],
                received.at[c, t],
                {"pool": p, "tensor": other},
            )

        def arrival(c, j):
            other = lax.rem(t + j, tensor)
            return remote(
                outgoing.at[c, other],
                incoming.at[c, other],
                sent.at[c, j],
                received.at[c, other],
                {"pool": p, "tensor": other},
            )

        for c in range(split):

            def columns(i):
                near = pl.multiple_of(i * chunk, chunk)
                product = jnp.dot(
                    left, weight[:, pl.ds(c * wide + near, chunk)], preferred_element_type=F32
                )
                for q in range(pool):
                    part[c, q, :, pl.ds(near, chunk)] = product[q * half : (q + 1) * half, :]

            each(0, wide // chunk, columns)
            swap(c).start()
        for c in range(split):
            swap(c).wait_recv()
            peer[c] = peer[c] + part[c, p]
            for index in range(tensor):
                outgoing[c, index] = peer[c, index * rows : (index + 1) * rows, :].astype(BF16)
            each(1, tensor, lambda j: copy(c, j).start())
            incoming[c, t] = outgoing[c, t]
        totals = []
        for c in range(split):
            each(1, tensor, lambda j: arrival(c, j).wait_recv())
            total = incoming[c, 0].astype(F32)
            for index in range(1, tensor):
                total = total + incoming[c, index].astype(F32)
            totals.append(total)

        def finish():
            for c in range(split):
                swap(c).wait_send()
                each(1, tensor, lambda j: copy(c, j).wait_send())

        return jnp.concatenate(totals, axis=1), finish

    split = ag1.shape[0]
    chunk = math.gcd(width // split, 512)
    half = tensor * rows

    def offer(buffer, values):
        wide = width // split
        for c in range(split):
            buffer[c, me] = values[:, c * wide : (c + 1) * wide].astype(BF16)

    hidden = hidden_ref[...].astype(F32)
    offer(ag1, rms_scale(hidden, input_gain_ref[...]))

    slot_row = slot_ref[...]
    length_row = length_ref[...]
    wide = devices * SLOTS
    scatter_hot = (
        lax.broadcasted_iota(jnp.int32, (wide, requests), 0) == slot_row
    ).astype(F32).astype(BF16)
    eye = lax.broadcasted_iota(jnp.int32, (requests, requests), 0) == lax.broadcasted_iota(
        jnp.int32, (requests, requests), 1
    )
    slot_col = jnp.sum(
        jnp.where(eye, jnp.broadcast_to(slot_row, (requests, requests)), 0).astype(F32),
        axis=1,
        keepdims=True,
    ).astype(jnp.int32)
    gather_hot = (
        lax.broadcasted_iota(jnp.int32, (requests, wide), 1) == slot_col
    ).astype(F32).astype(BF16)
    span = 2 * SLOTS
    place_id = lax.rem(lax.broadcasted_iota(jnp.int32, (span, requests), 0), SLOTS)
    slot_wide = jnp.broadcast_to(slot_row, (span, requests))
    length_wide = jnp.broadcast_to(length_row, (span, requests)).astype(F32)
    base = me * SLOTS
    slot_length = jnp.sum(
        jnp.where(slot_wide == base + place_id, length_wide, 0.0), axis=1, keepdims=True
    )
    slot_offset = jnp.sum(
        jnp.where((slot_wide >= base) & (slot_wide < base + place_id), length_wide, 0.0),
        axis=1,
        keepdims=True,
    )
    angles = slot_length * frequency_ref[...]
    cosine = jnp.cos(angles)
    lane = lax.broadcasted_iota(jnp.int32, (span, head_dim), 1)
    sine_part = jnp.where(lane < head_dim // 2, -jnp.sin(angles), jnp.sin(angles))
    pool_tokens = kc.shape[0]
    token = lax.broadcasted_iota(jnp.int32, (span, pool_tokens), 1).astype(F32)
    inside = jnp.where(
        (token >= slot_offset) & (token < slot_offset + slot_length), 1.0, 0.0
    )

    def turn(values, scale, copies):
        scaled = rms_scale(values, scale)
        return scaled * jnp.tile(cosine, (copies, 1)) + pltpu.roll(
            scaled, head_dim // 2, 1
        ) * jnp.tile(sine_part, (copies, 1))

    pl.semaphore_wait(barrier, devices - 1)
    for load in loads[:3]:
        load.wait()

    def turned(left, weight, at):
        return lax.dot_general(
            left, weight[:, at], (((1,), (1,)), ((), ())), preferred_element_type=F32
        )

    def project(i, carry):
        at = pl.ds(pl.multiple_of(i * chunk, chunk), chunk)
        left = xs[:, at].astype(BF16)
        return tuple(
            acc + product
            for acc, product in zip(
                carry,
                (
                    jnp.dot(left, qw[at, :], preferred_element_type=F32),
                    turned(left, kw, at),
                    turned(left, vw, at),
                ),
            )
        )

    (query_part, key_part, value_part), finish = gather(
        ag1,
        ag1_s,
        ag1_r,
        1,
        project,
        (
            jnp.zeros((requests, query_cols), F32),
            jnp.zeros((requests, key_cols), F32),
            jnp.zeros((requests, key_cols), F32),
        ),
    )

    done = [finish]

    def shift(count, amount):
        low = lax.broadcasted_iota(jnp.int32, (count, head_dim), 0)
        high = lax.broadcasted_iota(jnp.int32, (count, head_dim), 1)
        return (low + amount == high).astype(F32).astype(BF16)

    kv_part = jnp.dot(
        key_part.astype(BF16), shift(key_cols, 0), preferred_element_type=F32
    ) + jnp.dot(value_part.astype(BF16), shift(key_cols, key_cols), preferred_element_type=F32)
    slots[:, :query_cols] = jnp.dot(
        scatter_hot, query_part.astype(BF16), preferred_element_type=F32
    )
    slots[:, query_cols:] = jnp.dot(
        scatter_hot, kv_part.astype(BF16), preferred_element_type=F32
    )
    for index in range(devices):
        to_owner[index] = slots[index * SLOTS : (index + 1) * SLOTS, :].astype(BF16)
    done.append(exchange(to_owner, at_owner, a1_s, a1_r))

    for index in range(devices):
        arrived = at_owner[index].astype(F32)
        for j in range(heads_here):
            at = (index * heads_here + j) * SLOTS
            qs[at : at + SLOTS, :] = arrived[:, j * head_dim : (j + 1) * head_dim]
        at = (index // per_kv) * span
        lanes = (index % per_kv) * head_dim
        kvs[at : at + SLOTS, lanes : lanes + head_dim] = arrived[:, query_cols:]
        kvs[at + SLOTS : at + span, lanes : lanes + head_dim] = arrived[:, query_cols:]

    low = lax.broadcasted_iota(jnp.int32, (per_kv * head_dim, head_dim), 0)
    high = lax.broadcasted_iota(jnp.int32, (per_kv * head_dim, head_dim), 1)
    piece = lax.div(low, head_dim)
    inner = lax.rem(low, head_dim)
    key_hot = ((inner < key_cols) & (piece * key_cols + inner == high)).astype(F32).astype(BF16)
    value_hot = (
        ((inner >= key_cols) & (inner < 2 * key_cols) & (piece * key_cols + inner - key_cols == high))
        .astype(F32)
        .astype(BF16)
    )
    pieces = kvs[...].astype(BF16)
    key_new = turn(
        jnp.dot(pieces, key_hot, preferred_element_type=F32), key_gain_ref[...], kv_count
    ).astype(BF16)
    value_new = jnp.dot(pieces, value_hot, preferred_element_type=F32)
    scale_factor = 1.0 / math.sqrt(head_dim)
    block = group * SLOTS
    copies = block // span
    allowed = jnp.tile(inside, (copies, 1)) > 0.5
    for load in loads[3:5]:
        load.wait()
    for k in range(kv_count):
        query = turn(qs[k * block : (k + 1) * block, :], query_gain_ref[...], copies).astype(BF16)
        lanes = slice(k * head_dim, (k + 1) * head_dim)
        scores = (
            lax.dot_general(
                query, kc[:, lanes], (((1,), (1,)), ((), ())), preferred_element_type=F32
            )
            * scale_factor
        )
        own_key = jnp.tile(key_new[k * span : (k + 1) * span, :].astype(F32), (copies, 1))
        own_value = jnp.tile(value_new[k * span : (k + 1) * span, :], (copies, 1))
        own_score = jnp.sum(query.astype(F32) * own_key, axis=1, keepdims=True) * scale_factor
        scores = jnp.where(allowed, scores, -1e30)
        largest = jnp.maximum(jnp.max(scores, axis=1, keepdims=True), own_score)
        weights = jnp.exp(scores - largest)
        own_weight = jnp.exp(own_score - largest)
        denominator = jnp.sum(weights, axis=1, keepdims=True) + own_weight
        summed = jnp.dot(weights.astype(BF16), vc[:, lanes], preferred_element_type=F32)
        summed = summed + own_weight.astype(BF16).astype(F32) * own_value
        ho[k * block : (k + 1) * block, :] = summed / denominator
    for index in range(devices):
        for j in range(heads_here):
            at = (index * heads_here + j) * SLOTS
            to_home[index, :, j * head_dim : (j + 1) * head_dim] = ho[at : at + SLOTS, :].astype(BF16)
    done.append(exchange(to_home, at_home, a2_s, a2_r))
    for index in range(devices):
        back[index * SLOTS : (index + 1) * SLOTS, :] = at_home[index].astype(F32)
    head_rows = jnp.dot(
        gather_hot, back[...].astype(BF16), preferred_element_type=F32
    ).astype(BF16)

    loads[5].wait()
    total, finish = scatter_sum(head_rows, ow, part1, peer1, out1, in1, rs1_s, rs1_r)
    done.append(finish)
    mixed = (total + hidden).astype(BF16)
    both_ref[0] = mixed.astype(F32)
    offer(ag2, rms_scale(mixed, post_gain_ref[...]))
    loads[6].wait()
    loads[7].wait()

    def expand(i, carry):
        at = pl.ds(pl.multiple_of(i * chunk, chunk), chunk)
        left = xs[:, at].astype(BF16)
        return tuple(
            acc + turned(left, w, at)
            for acc, w in zip(carry, (gw, uw))
        )

    (gate_part, up_part), finish = gather(
        ag2,
        ag2_s,
        ag2_r,
        2,
        expand,
        (jnp.zeros((requests, hidden_units), F32), jnp.zeros((requests, hidden_units), F32)),
    )
    done.append(finish)
    activated = (gate_part / (1.0 + jnp.exp(-gate_part)) * up_part).astype(BF16)
    loads[8].wait()
    total, finish = scatter_sum(activated, dw, part2, peer2, out2, in2, rs2_s, rs2_r)
    done.append(finish)
    both_ref[1] = both_ref[0] + total
    for finish in done:
        finish()


def fused(pool, tensor, *operands):
    (
        hidden,
        input_gain,
        query_weight,
        key_weight,
        value_weight,
        query_gain,
        key_gain,
        output_weight,
        post_gain,
        gate_weight,
        up_weight,
        down_weight,
        key_cache,
        value_cache,
        lengths,
        request_slot,
    ) = operands
    devices = pool * tensor
    rows, width = hidden.shape
    head_dim = query_gain.shape[0]
    query_cols = query_weight.shape[1]
    key_cols = key_weight.shape[1]
    heads_here = query_cols // head_dim
    kv_count = devices * key_cols // head_dim
    per_kv = devices // kv_count
    requests = devices * rows
    half_width = head_dim // 2
    frequency = theta ** (-np.arange(half_width) * 2.0 / head_dim)
    frequency = np.concatenate([frequency, frequency])[None, :].astype(np.float32)
    heavy = (
        query_weight,
        key_weight.T,
        value_weight.T,
        output_weight,
        gate_weight.T,
        up_weight.T,
        down_weight,
        key_cache,
        value_cache,
    )
    dma = pltpu.SemaphoreType.DMA
    sent_cols = query_cols + head_dim
    sums = [
        pltpu.VMEM((SPLIT, pool, tensor * rows, width // SPLIT), F32),
        pltpu.VMEM((SPLIT, tensor * rows, width // SPLIT), F32),
        pltpu.VMEM((SPLIT, tensor, rows, width // SPLIT), BF16),
        pltpu.VMEM((SPLIT, tensor, rows, width // SPLIT), BF16),
    ]
    scratch = (
        [pltpu.VMEM(w.shape, w.dtype) for w in heavy]
        + [pltpu.VMEM((SPLIT, devices, rows, width // SPLIT), BF16)] * 2
        + [
            pltpu.VMEM((requests, width), F32),
            pltpu.VMEM((devices * SLOTS, sent_cols), F32),
            pltpu.VMEM((devices, SLOTS, sent_cols), BF16),
            pltpu.VMEM((devices, SLOTS, sent_cols), BF16),
            pltpu.VMEM((devices * heads_here * SLOTS, head_dim), F32),
            pltpu.VMEM((kv_count * 2 * SLOTS, per_kv * head_dim), F32),
            pltpu.VMEM((devices * heads_here * SLOTS, head_dim), F32),
            pltpu.VMEM((devices, SLOTS, query_cols), BF16),
            pltpu.VMEM((devices, SLOTS, query_cols), BF16),
            pltpu.VMEM((devices * SLOTS, query_cols), F32),
        ]
        + sums
        + sums
        + [dma((len(heavy),))]
        + [dma((SPLIT, 2 * tensor)), dma((SPLIT, devices))] * 2
        + [dma((devices,)), dma((devices,))] * 2
        + [dma((SPLIT, tensor)), dma((SPLIT, tensor + 1))] * 2
    )
    vmem = pl.BlockSpec(memory_space=pltpu.VMEM)
    hbm = pl.BlockSpec(memory_space=pl.ANY)
    both = jax.ShapeDtypeStruct((2, *hidden.shape), F32)
    both = pl.pallas_call(
        functools.partial(step_kernel, pool, tensor),
        out_shape=both,
        in_specs=[vmem] * 8 + [hbm] * len(heavy),
        out_specs=vmem,
        scratch_shapes=scratch,
        compiler_params=pltpu.CompilerParams(
            collective_id=0, has_side_effects=True, vmem_limit_bytes=62 * 1024 * 1024
        ),
    )(
        hidden,
        input_gain[None, :],
        query_gain[None, :],
        key_gain[None, :],
        post_gain[None, :],
        lengths[None, :],
        request_slot[None, :],
        frequency,
        *heavy,
    )
    return both[0].astype(hidden.dtype), both[1].astype(hidden.dtype)


def dispatch(pool, tensor, *operands):
    query_cols = operands[2].shape[1]
    key_cols = operands[3].shape[1]
    head_dim = operands[5].shape[0]
    whole_heads = query_cols % head_dim == 0 and head_dim % key_cols == 0
    lanes = operands[0].shape[1] % (SPLIT * 512) == 0
    if pool == 2 and lanes and whole_heads and 2 * key_cols <= head_dim:
        return fused(pool, tensor, *operands)
    return on_device(*operands)


def solution(mesh):
    placed = (
        P(("groups", "pool", "tensor"), None),
        P(),
        P(None, ("pool", "tensor")),
        P(None, ("pool", "tensor")),
        P(None, ("pool", "tensor")),
        P(),
        P(),
        P(("pool", "tensor"), None),
        P(),
        P(None, ("pool", "tensor")),
        P(None, ("pool", "tensor")),
        P(("pool", "tensor"), None),
        P(("groups", "pool", "tensor"), None),
        P(("groups", "pool", "tensor"), None),
        P("groups"),
        P("groups"),
    )
    return jax.shard_map(
        functools.partial(dispatch, mesh.shape["pool"], mesh.shape["tensor"]),
        mesh=mesh,
        in_specs=placed,
        out_specs=(P(("groups", "pool", "tensor"), None), P(("groups", "pool", "tensor"), None)),
        check_vma=False,
    )
```
